32 devices in a mesh: pw: 2 (over y), tile: 16 (over z, x, core).
Axes of the slice: x: 2, y: 2, z: 4, core: 2. Of those that a mesh axis runs over, the one named last changes fastest.
Arguments:
- mask_tiles: float32 [4, 256, 4096], P(None, None, 'tile'), may hold values from 0 to 1
- target_print: float32 [4, 256, 4096], P(None, None, 'tile'), may hold values from 0 to 1
- geometry_flags: int32 [4, 16], P(None, 'tile'), may hold values from 0 to 1, as said below
- kernel_taps: float32 [2, 12, 4, 129], P('pw'), may hold values from -0.5 to 0.5
- dose_factor: float32 [2], P('pw'), may hold values from 0.7 to 1.4
Outputs:
- mask_gradient: float32 [4, 256, 4096], P(None, 'pw', 'tile')
The draws below stay inside these ranges and needn't reach their ends.
Inputs may be any that keep to these rules, and one draw needn't show every extreme that they name: `geometry_flags`: every tile column has at most 1 tiles with geometry, and some column has exactly 1.
All inputs are finite; a program needn't handle non-finite values.
Results may differ from the reference program's by a relative error of at most 0.0089.
Values may be sent and summed in bfloat16 or wider, within the bound.
A program may use at most 128 MiB of HBM per device.

```python
import jax
import jax.numpy as jnp
from jax import lax

TILE = 256
AMBIT = 64
KERNELS = 12
TILE_ROWS = 4
ACTIVE_MOST = 1
TAPS = 129
EXTENT = 384
COLUMNS = 16
CONDITIONS = 2
HEIGHT = 1024
WIDTH = 4096


def draw_geometry_flags(key, part):
    key_heavy = jax.random.fold_in(key, 11)
    key_forced = jax.random.fold_in(key, 12)
    key_light = jax.random.fold_in(key, 13)
    key_scores = jax.random.fold_in(key, 14)
    heavy_column = jax.random.randint(key_heavy, (COLUMNS,), 0, 4) == 0
    forced = jax.random.randint(key_forced, (), 0, COLUMNS)
    heavy_column = heavy_column | (jnp.arange(COLUMNS) == forced)
    light_count = jax.random.randint(key_light, (COLUMNS,), 0, ACTIVE_MOST // 2 + 2)
    light_count = jnp.minimum(light_count, ACTIVE_MOST)
    counts = jnp.where(heavy_column, ACTIVE_MOST, light_count)
    scores = jax.random.randint(key_scores, (TILE_ROWS, COLUMNS), 0, 1 << 20) * TILE_ROWS + jnp.arange(TILE_ROWS)[:, None]
    ordering = jnp.argsort(scores, axis=0, stable=True)
    ranking = jnp.argsort(ordering, axis=0, stable=True)
    return (ranking < counts[None, :]).astype(jnp.int32)


def block_scale(own_key, shape, split, low, largest):
    def one(axis_at, parts):
        heights = jax.random.uniform(jax.random.fold_in(jax.random.fold_in(own_key, 6), axis_at), (parts,), jnp.float32, low / len(split), largest / len(split))
        return jnp.repeat(jnp.exp(heights), shape[axis_at] // parts).reshape((-1,) + (1,) * (len(shape) - axis_at - 1))

    level = one(*split[0])
    for cut in split[1:]:
        level = level * one(*cut)
    return level


def scatter_about(own_key, shape, scale, most, pieces=(), kind=jnp.bfloat16):
    values = scale * jax.random.normal(own_key, shape, jnp.float32)
    if pieces:
        values = values * block_scale(own_key, shape, pieces, -0.22, 0.18)
    return jnp.clip(values, -most, most).astype(kind)


def setup_inputs(seed: int = 0) -> dict:
    seeds = jax.random.split(jax.random.key(seed), 6)
    mask_tiles = jnp.clip(1.0 * jax.random.uniform(seeds[0], (TILE_ROWS, TILE, WIDTH), jnp.float32) ** block_scale(seeds[0], (TILE_ROWS, TILE, WIDTH), ((2, 16),), -0.2, 0.2), 0.0, 1.0)
    target_print = jnp.clip(1.0 * jax.random.uniform(seeds[1], (TILE_ROWS, TILE, WIDTH), jnp.float32) ** block_scale(seeds[1], (TILE_ROWS, TILE, WIDTH), ((2, 16),), -0.2, 0.2), 0.0, 1.0)
    geometry_flags = draw_geometry_flags(jax.random.fold_in(seeds[5], 71), 0)
    kernel_taps = scatter_about(seeds[3], (CONDITIONS, KERNELS, 4, TAPS), TAPS ** -0.5, 0.5, ((0, 2),), jnp.float32)
    dose_factor = jnp.clip(0.7 + 0.7 * jax.random.uniform(seeds[4], (CONDITIONS,), jnp.float32) ** block_scale(seeds[4], (CONDITIONS,), ((0, 2),), -0.2, 0.2), 0.7, 1.4)
    return dict(mask_tiles=mask_tiles, target_print=target_print, geometry_flags=geometry_flags, kernel_taps=kernel_taps, dose_factor=dose_factor)


STEEP = 4.0
THRESHOLD = 1.3
LOSS_WEIGHT = 4.0


def skew_band(taps_low):
    lead = taps_low.shape[:-1]
    padded = jnp.pad(taps_low, [(0, 0)] * len(lead) + [(0, EXTENT + 1 - TAPS)])
    repeated = jnp.tile(padded, (1,) * len(lead) + (TILE,))
    return repeated[..., :TILE * EXTENT].reshape(lead + (TILE, EXTENT))


def build_tables(taps_one):
    bands = skew_band(taps_one.astype(jnp.bfloat16))
    row_real = bands[:, 0]
    row_imag = bands[:, 1]
    col_real = bands[:, 2]
    col_imag = bands[:, 3]
    fwd_rows = bands[:, 0:2]
    fwd_cols = jnp.concatenate([jnp.concatenate([col_real, -col_imag], axis=2), jnp.concatenate([col_imag, col_real], axis=2)], axis=1)
    adj_cols = jnp.concatenate([jnp.concatenate([col_real, col_imag], axis=2), jnp.concatenate([col_imag, -col_real], axis=2)], axis=1)
    adj_rows = jnp.stack([row_real, -row_imag], axis=2)
    return fwd_rows, fwd_cols, adj_cols, adj_rows


def tile_gradient(window, goal_tile, live_weight, dose_value, tables):
    fwd_rows, fwd_cols, adj_cols, adj_rows = tables
    partial_field = jnp.einsum("kcte,ef->ktcf", fwd_rows.astype(jnp.float32), window.astype(jnp.float32))
    partial_field = partial_field.reshape(KERNELS, TILE, 2 * EXTENT).astype(jnp.bfloat16)
    field_all = jnp.einsum("ktf,ksf->kts", partial_field.astype(jnp.float32), fwd_cols.astype(jnp.float32))
    real_field = field_all[:, :, :TILE]
    imag_field = field_all[:, :, TILE:]
    intensity = (dose_value / KERNELS) * jnp.sum(real_field * real_field + imag_field * imag_field, axis=0)
    resist = jax.nn.sigmoid(STEEP * (intensity - THRESHOLD))
    sensitivity = live_weight * LOSS_WEIGHT * 2.0 * (resist - goal_tile) * resist * (1.0 - resist) * STEEP * dose_value / KERNELS
    weighted = (field_all * jnp.concatenate([sensitivity, sensitivity], axis=1)[None]).astype(jnp.bfloat16)
    adjoint = jnp.einsum("kts,ksf->ktf", weighted.astype(jnp.float32), adj_cols.astype(jnp.float32)).astype(jnp.bfloat16)
    adjoint = adjoint.reshape(KERNELS, TILE, 2, EXTENT)
    return 2.0 * jnp.einsum("ktce,ktcf->ef", adj_rows.astype(jnp.float32), adjoint.astype(jnp.float32))


def reference(mask_tiles, target_print, geometry_flags, kernel_taps, dose_factor):
    mask_image = mask_tiles.astype(jnp.bfloat16).reshape(HEIGHT, WIDTH)
    padded = jnp.pad(mask_image, AMBIT)
    goal_image = target_print.reshape(HEIGHT, WIDTH)
    present = geometry_flags.reshape(-1).astype(jnp.int32)
    slot_count = ACTIVE_MOST * COLUMNS
    position = (jnp.cumsum(present) - 1).astype(jnp.int32)
    live_count = jnp.sum(present).astype(jnp.int32)
    target_slot = jnp.where(present > 0, position, slot_count).astype(jnp.int32)
    slot_tile = jnp.zeros((slot_count,), jnp.int32).at[target_slot].set(jnp.arange(present.shape[0], dtype=jnp.int32), mode="drop")
    live_slots = (jnp.arange(slot_count, dtype=jnp.int32) < live_count).astype(jnp.float32)

    def one_condition(summed, inputs):
        taps_one, dose_value = inputs
        tables = build_tables(taps_one)

        def add_tile(slot_number, buffer):
            tile_id = slot_tile[slot_number]
            row_start = ((tile_id // COLUMNS) * TILE).astype(jnp.int32)
            col_start = ((tile_id % COLUMNS) * TILE).astype(jnp.int32)
            window = lax.dynamic_slice(padded, (row_start, col_start), (EXTENT, EXTENT))
            goal_tile = lax.dynamic_slice(goal_image, (row_start, col_start), (TILE, TILE))
            tile_grad = tile_gradient(window, goal_tile, live_slots[slot_number], dose_value, tables)
            current = lax.dynamic_slice(buffer, (row_start, col_start), (EXTENT, EXTENT))
            return lax.dynamic_update_slice(buffer, current + tile_grad, (row_start, col_start))

        buffer = lax.fori_loop(0, slot_count, add_tile, jnp.zeros((HEIGHT + 2 * AMBIT, WIDTH + 2 * AMBIT), jnp.float32))
        return summed + buffer[AMBIT:AMBIT + HEIGHT, AMBIT:AMBIT + WIDTH], None

    summed, unused = lax.scan(one_condition, jnp.zeros((HEIGHT, WIDTH), jnp.float32), (kernel_taps, dose_factor))
    return summed.reshape(TILE_ROWS, TILE, WIDTH)
```

```python
import jax
import jax.numpy as jnp
from jax import lax
from jax.experimental import pallas as pl
from jax.experimental.pallas import tpu as pltpu
from jax.sharding import PartitionSpec as P

STEEP = 4.0
THRESHOLD = 1.3
LOSS_WEIGHT = 4.0
LANES = 128
F32 = jnp.float32
BF16 = jnp.bfloat16


def low_lanes(rows, half):
    return lax.broadcasted_iota(jnp.int32, (rows, LANES), 1) < half


def gradient_kernel(
    sizes, mask_hbm, goal_hbm, flags, taps, dose, halos, center, rims,
    mask_f32, goal_f32, row_bands, row_bands_t, col_a, col_b,
    fields_in, fields, intensity, adjoint, local_sem,
):
    pw_count, tile_rows, tile, kernels, ambit = sizes
    height = tile_rows * tile
    extent = tile + 2 * ambit
    own_rows = tile // pw_count
    edge_rows = min(own_rows, ambit)
    pack_rows = own_rows + edge_rows

    mask_copy = pltpu.make_async_copy(mask_hbm, mask_f32.at[ambit:ambit + height], local_sem.at[0])
    mask_copy.start()
    zero_rows = jnp.zeros((ambit, tile), F32)
    mask_f32[0:ambit, :] = zero_rows
    mask_f32[ambit + height:, :] = zero_rows
    live_row = sum(g * flags[g] for g in range(tile_rows))
    live = sum(flags[g] for g in range(tile_rows)).astype(F32)
    window = pl.ds(pl.multiple_of(live_row * tile, tile), extent)
    goal_copy = pltpu.make_async_copy(goal_hbm.at[live_row], goal_f32, local_sem.at[1])
    goal_copy.start()

    def band(k, which):
        row = jnp.broadcast_to(taps[k, which:which + 1, :], (LANES, 2 * LANES))
        return pltpu.roll(row, 0, 1, stride=1, stride_axis=0)

    def build(k, carry):
        row_real, row_imag = band(k, 0).astype(BF16), band(k, 1).astype(BF16)
        col_real, col_imag = band(k, 2), band(k, 3)
        row_bands[k, 0:LANES, :] = row_real
        row_bands[k, LANES:, :] = row_imag
        row_bands_t[k, :, 0:LANES] = row_real.T
        row_bands_t[k, :, LANES:] = row_imag.T
        col_a[k, 0:LANES, :] = col_real.astype(BF16)
        col_a[k, LANES:, :] = col_imag.astype(BF16)
        col_b[k, 0:LANES, :] = (-col_imag).astype(BF16)
        col_b[k, LANES:, :] = col_real.astype(BF16)
        return carry

    lax.fori_loop(0, kernels, build, 0)

    mask_copy.wait()
    low = low_lanes(extent, ambit)
    turned_a = pltpu.roll(mask_f32[window, 0:LANES], ambit, 1)
    turned_b = pltpu.roll(mask_f32[window, LANES:], ambit, 1)
    rim = jnp.where(low, turned_b, turned_a)
    halo = halos[window, :].astype(F32)

    def row_stage(block, at):
        both = jnp.concatenate([block[0:2 * LANES], block[LANES:3 * LANES]], axis=1)

        def one(k):
            z = jnp.dot(row_bands[k], both, preferred_element_type=F32).astype(BF16)
            for part in range(2):
                for i in range(2):
                    fields_in[k, part, i * LANES:(i + 1) * LANES, at * LANES:(at + 1) * LANES] = (
                        z[part * LANES:(part + 1) * LANES, i * LANES:(i + 1) * LANES])

        for k in range(kernels):
            one(k)

    row_stage(jnp.where(low, turned_a, turned_b).astype(BF16), 1)
    row_stage(jnp.where(low, halo, rim).astype(BF16), 0)
    row_stage(jnp.where(low, rim, halo).astype(BF16), 2)

    contract_last = (((1,), (1,)), ((), ()))
    intensity[...] = jnp.zeros_like(intensity)

    def column(k, carry):
        total = None
        for part, table in ((0, col_a), (1, col_b)):
            lhs = jnp.concatenate(
                [fields_in[k, part, :, 0:2 * LANES], fields_in[k, part, :, LANES:3 * LANES]], axis=0)
            term = lax.dot_general(lhs, table[k], contract_last, preferred_element_type=F32)
            total = term if total is None else total + term
        fields[k] = total
        real, imag = total[:, :LANES], total[:, LANES:]
        intensity[...] += real * real + imag * imag
        return carry

    lax.fori_loop(0, kernels, column, 0)

    goal_copy.wait()
    dose_value = dose[0]
    goal = goal_f32[...]
    for j in range(2):
        rows = slice(j * tile, (j + 1) * tile)
        resist = jax.nn.sigmoid(STEEP * (dose_value / kernels * intensity[rows, :] - THRESHOLD))
        wanted = goal[:, j * LANES:(j + 1) * LANES]
        factor = live * LOSS_WEIGHT * 2.0 * STEEP * dose_value / kernels
        intensity[rows, :] = factor * (resist - wanted) * resist * (1.0 - resist)

    def adjoint_stage(k, carry):
        scale = intensity[...]
        weighted = (fields[k] * jnp.concatenate([scale, scale], axis=1)).astype(BF16)
        for part, table in ((0, col_a), (1, col_b)):
            wide = jnp.dot(weighted, table[k], preferred_element_type=F32)
            blocks = (wide[:tile, :LANES], wide[:tile, LANES:] + wide[tile:, :LANES], wide[tile:, LANES:])
            for b, block in enumerate(blocks):
                block = block.astype(BF16)
                for i in range(2):
                    adjoint[b, k, part * LANES:(part + 1) * LANES, i * LANES:(i + 1) * LANES] = (
                        block[i * LANES:(i + 1) * LANES])
        return carry

    lax.fori_loop(0, kernels, adjoint_stage, 0)

    turned = []
    for b in range(3):
        total = jnp.zeros((2 * LANES, 2 * LANES), F32)
        for k in range(kernels):
            total += jnp.dot(row_bands_t[k], adjoint[b, k], preferred_element_type=F32)
        total = 2.0 * total
        rows = jnp.concatenate(
            [total[:LANES, :LANES], total[LANES:, :LANES] + total[:LANES, LANES:], total[LANES:, LANES:]], axis=0)
        turned.append(pltpu.roll(rows, ambit, 1))
    blocks = (jnp.where(low, turned[0], turned[1]), jnp.where(low, turned[1], turned[2]),
              jnp.where(low, turned[2], turned[0]))
    flag_rows = jnp.concatenate(
        [jnp.full((1, LANES), flags[g].astype(F32)) for g in range(tile_rows)]
        + [jnp.zeros((16 - tile_rows, LANES), F32)], axis=0)
    for q in range(pw_count):
        first = ambit + q * own_rows
        if q * own_rows < ambit:
            edge = ambit + tile + q * own_rows
        else:
            edge = max(q * own_rows - (tile - ambit), 0)
        for b, block in enumerate(blocks):
            main = block[first:first + own_rows].astype(BF16)
            side = block[edge:edge + edge_rows].astype(BF16)
            if b < 2:
                center[q, 0:own_rows, b * LANES:(b + 1) * LANES] = main
                center[q, own_rows:, b * LANES:(b + 1) * LANES] = side
            else:
                rims[q, 0:own_rows, :] = main
                rims[q, own_rows:pack_rows, :] = side
                rims[q, pack_rows:, :] = flag_rows.astype(BF16)


def gather_kernel(sizes, flags, place, own_center, *refs):
    pw_count, tile_rows, tile, ambit = sizes
    centers, lefts, rights = refs[:pw_count - 1], refs[pw_count - 1:2 * pw_count - 1], refs[2 * pw_count - 1:-1]
    out_ref = refs[-1]
    own_rows = tile // pw_count
    edge_rows = min(own_rows, ambit)
    pack_rows = own_rows + edge_rows
    p = place[0]
    total = own_center[p].astype(F32)
    for ref in centers:
        total += ref[...].astype(F32)
    left, right = lefts[0][...].astype(F32), rights[0][...].astype(F32)
    left_sum = sum(ref[0:pack_rows, :].astype(F32) for ref in lefts)
    right_sum = sum(ref[0:pack_rows, :].astype(F32) for ref in rights)
    pack_low = low_lanes(pack_rows, ambit)
    left_sum = jnp.where(pack_low, left_sum, 0.0)
    right_sum = jnp.where(pack_low, 0.0, right_sum)
    is_low = jnp.where(p * own_rows < ambit, 1.0, 0.0).astype(F32)
    is_high = jnp.where((p + 1) * own_rows > tile - ambit, 1.0, 0.0).astype(F32)
    halves = ((total[:, :LANES], left_sum, left), (total[:, LANES:], right_sum, right))

    def flag_of(kind, g):
        if g < 0 or g >= tile_rows:
            return None
        if kind is None:
            return flags[g].astype(F32)
        return kind[pack_rows + g:pack_rows + g + 1, :]

    for b, (own, rim, rim_flags) in enumerate(halves):
        lanes = slice(b * LANES, (b + 1) * LANES)
        for g in range(tile_rows):
            out_ref[g, :, lanes] = (
                flag_of(None, g) * own[:own_rows] + flag_of(rim_flags, g) * rim[:own_rows])
            for at, switch, source in ((0, is_low, g - 1), (own_rows - edge_rows, is_high, g + 1)):
                if 0 <= source < tile_rows:
                    out_ref[g, at:at + edge_rows, lanes] += switch * (
                        flag_of(None, source) * own[own_rows:] + flag_of(rim_flags, source) * rim[own_rows:])


def solution(mesh):
    pw_count, tile_count = mesh.shape["pw"], mesh.shape["tile"]

    def on_device(mask_tiles, target_print, geometry_flags, kernel_taps, dose_factor):
        tile_rows, tile, _ = mask_tiles.shape
        kernels, kinds, tap_count = kernel_taps.shape[1:]
        ambit = (tap_count - 1) // 2
        height, extent = tile_rows * tile, tile + 2 * ambit
        own_rows = tile // pw_count
        pack_rows = own_rows + min(own_rows, ambit)
        wide = 2 * LANES
        vmem = pl.BlockSpec(memory_space=pltpu.VMEM)
        smem = pl.BlockSpec(memory_space=pltpu.SMEM)
        anywhere = pl.BlockSpec(memory_space=pl.ANY)
        p = lax.axis_index("pw")
        taps = jnp.pad(kernel_taps[0], ((0, 0), (0, 8 - kinds), (0, wide - tap_count)))
        flags = geometry_flags.reshape(tile_rows)
        mask = mask_tiles.reshape(height, tile)
        right_way = [(i, i + 1) for i in range(tile_count - 1)]
        left_way = [(j, i) for i, j in right_way]
        before = lax.ppermute(mask[:, tile - ambit:].astype(BF16), "tile", right_way)
        after = lax.ppermute(mask[:, :ambit].astype(BF16), "tile", left_way)
        halos = jnp.pad(jnp.concatenate([before, after], axis=1), ((ambit, ambit), (0, 0)))

        def gradient(*refs):
            gradient_kernel((pw_count, tile_rows, tile, kernels, ambit), *refs)

        def gather(*refs):
            gather_kernel((pw_count, tile_rows, tile, ambit), *refs)

        center, rims = pl.pallas_call(
            gradient,
            out_shape=(
                jax.ShapeDtypeStruct((pw_count, pack_rows, tile), BF16),
                jax.ShapeDtypeStruct((pw_count, pack_rows + 16, LANES), BF16),
            ),
            in_specs=[anywhere, anywhere, smem, vmem, smem, vmem],
            out_specs=(vmem, vmem),
            scratch_shapes=[
                pltpu.VMEM((height + 2 * ambit, tile), F32),
                pltpu.VMEM((tile, tile), F32),
                pltpu.VMEM((kernels, wide, wide), BF16),
                pltpu.VMEM((kernels, wide, wide), BF16),
                pltpu.VMEM((kernels, wide, wide), BF16),
                pltpu.VMEM((kernels, wide, wide), BF16),
                pltpu.VMEM((kernels, 2, tile, extent), BF16),
                pltpu.VMEM((kernels, 2 * tile, wide), F32),
                pltpu.VMEM((2 * tile, LANES), F32),
                pltpu.VMEM((3, kernels, wide, wide), BF16),
                pltpu.SemaphoreType.DMA((2,)),
            ],
            compiler_params=pltpu.CompilerParams(vmem_limit_bytes=48 * 1024 * 1024),
        )(mask, target_print, flags, taps, dose_factor, halos)

        def device(q, column):
            return q * tile_count + column

        def moved(block, shift, step):
            pairs = [
                (device(q, i), device((q + step) % pw_count, i + shift))
                for q in range(pw_count) for i in range(tile_count) if 0 <= i + shift < tile_count]
            return lax.ppermute(block, ("pw", "tile"), pairs)

        sent = [lax.rem(p + step, pw_count) for step in range(pw_count)]
        centers = [moved(center[sent[step]], 0, step) for step in range(1, pw_count)]
        lefts = [moved(rims[sent[step]], 1, step) for step in range(pw_count)]
        rights = [moved(rims[sent[step]], -1, step) for step in range(pw_count)]
        count = 1 + len(centers) + len(lefts) + len(rights)
        return pl.pallas_call(
            gather,
            out_shape=jax.ShapeDtypeStruct((tile_rows, own_rows, tile), F32),
            in_specs=[smem, smem] + [vmem] * count,
            out_specs=vmem,
        )(flags, p.reshape(1), center, *centers, *lefts, *rights)

    return jax.shard_map(
        on_device,
        mesh=mesh,
        in_specs=(
            P(None, None, "tile"),
            P(None, None, "tile"),
            P(None, "tile"),
            P("pw", None, None, None),
            P("pw"),
        ),
        out_specs=P(None, "pw", "tile"),
        check_vma=False,
    )
```

```python
import jax
import jax.numpy as jnp
from jax import lax
from jax.experimental import pallas as pl
from jax.experimental.pallas import tpu as pltpu
from jax.sharding import PartitionSpec as P

STEEP = 4.0
THRESHOLD = 1.3
LOSS_WEIGHT = 4.0
LANES = 128
MESH = pl.DeviceIdType.MESH
F32 = jnp.float32
BF16 = jnp.bfloat16


def low_lanes(rows, half):
    return lax.broadcasted_iota(jnp.int32, (rows, LANES), 1) < half


def gradient_kernel(
    sizes, mask_hbm, goal_hbm, flags, taps, dose, place, halos, center, rims,
    mask_f32, goal_f32, row_bands, row_bands_t, col_a, col_b,
    fields_in, fields, intensity, adjoint, local_sem,
):
    pw_count, tile_rows, tile, kernels, ambit = sizes
    height = tile_rows * tile
    extent = tile + 2 * ambit
    own_rows = tile // pw_count
    edge_rows = min(own_rows, ambit)
    pack_rows = own_rows + edge_rows

    mask_copy = pltpu.make_async_copy(mask_hbm, mask_f32.at[ambit:ambit + height], local_sem.at[0])
    mask_copy.start()
    zero_rows = jnp.zeros((ambit, tile), F32)
    mask_f32[0:ambit, :] = zero_rows
    mask_f32[ambit + height:, :] = zero_rows
    live_row = sum(g * flags[g] for g in range(tile_rows))
    live = sum(flags[g] for g in range(tile_rows)).astype(F32)
    window = pl.ds(pl.multiple_of(live_row * tile, tile), extent)
    goal_copy = pltpu.make_async_copy(goal_hbm.at[live_row], goal_f32, local_sem.at[1])
    goal_copy.start()

    def band(k, which):
        row = jnp.broadcast_to(taps[k, which:which + 1, :], (LANES, 2 * LANES))
        return pltpu.roll(row, 0, 1, stride=1, stride_axis=0)

    def build(k, carry):
        row_real, row_imag = band(k, 0).astype(BF16), band(k, 1).astype(BF16)
        col_real, col_imag = band(k, 2), band(k, 3)
        row_bands[k, 0:LANES, :] = row_real
        row_bands[k, LANES:, :] = row_imag
        row_bands_t[k, :, 0:LANES] = row_real.T
        row_bands_t[k, :, LANES:] = row_imag.T
        col_a[k, 0:LANES, :] = col_real.astype(BF16)
        col_a[k, LANES:, :] = col_imag.astype(BF16)
        col_b[k, 0:LANES, :] = (-col_imag).astype(BF16)
        col_b[k, LANES:, :] = col_real.astype(BF16)
        return carry

    lax.fori_loop(0, kernels, build, 0)

    mask_copy.wait()
    low = low_lanes(extent, ambit)
    turned_a = pltpu.roll(mask_f32[window, 0:LANES], ambit, 1)
    turned_b = pltpu.roll(mask_f32[window, LANES:], ambit, 1)
    rim = jnp.where(low, turned_b, turned_a)
    halo = halos[window, :].astype(F32)

    def row_stage(block, at):
        both = jnp.concatenate([block[0:2 * LANES], block[LANES:3 * LANES]], axis=1)

        def one(k):
            z = jnp.dot(row_bands[k], both, preferred_element_type=F32).astype(BF16)
            for part in range(2):
                for i in range(2):
                    fields_in[k, part, i * LANES:(i + 1) * LANES, at * LANES:(at + 1) * LANES] = (
                        z[part * LANES:(part + 1) * LANES, i * LANES:(i + 1) * LANES])

        for k in range(kernels):
            one(k)

    row_stage(jnp.where(low, turned_a, turned_b).astype(BF16), 1)
    row_stage(jnp.where(low, halo, rim).astype(BF16), 0)
    row_stage(jnp.where(low, rim, halo).astype(BF16), 2)

    contract_last = (((1,), (1,)), ((), ()))
    intensity[...] = jnp.zeros_like(intensity)

    def column(k, carry):
        total = None
        for part, table in ((0, col_a), (1, col_b)):
            lhs = jnp.concatenate(
                [fields_in[k, part, :, 0:2 * LANES], fields_in[k, part, :, LANES:3 * LANES]], axis=0)
            term = lax.dot_general(lhs, table[k], contract_last, preferred_element_type=F32)
            total = term if total is None else total + term
        fields[k] = total
        real, imag = total[:, :LANES], total[:, LANES:]
        intensity[...] += real * real + imag * imag
        return carry

    lax.fori_loop(0, kernels, column, 0)

    goal_copy.wait()
    dose_value = dose[0]
    goal = goal_f32[...]
    for j in range(2):
        rows = slice(j * tile, (j + 1) * tile)
        resist = jax.nn.sigmoid(STEEP * (dose_value / kernels * intensity[rows, :] - THRESHOLD))
        wanted = goal[:, j * LANES:(j + 1) * LANES]
        factor = live * LOSS_WEIGHT * 2.0 * STEEP * dose_value / kernels
        intensity[rows, :] = factor * (resist - wanted) * resist * (1.0 - resist)

    def adjoint_stage(k, carry):
        scale = intensity[...]
        weighted = (fields[k] * jnp.concatenate([scale, scale], axis=1)).astype(BF16)
        for part, table in ((0, col_a), (1, col_b)):
            wide = jnp.dot(weighted, table[k], preferred_element_type=F32)
            blocks = (wide[:tile, :LANES], wide[:tile, LANES:] + wide[tile:, :LANES], wide[tile:, LANES:])
            for b, block in enumerate(blocks):
                block = block.astype(BF16)
                for i in range(2):
                    adjoint[b, k, part * LANES:(part + 1) * LANES, i * LANES:(i + 1) * LANES] = (
                        block[i * LANES:(i + 1) * LANES])
        return carry

    lax.fori_loop(0, kernels, adjoint_stage, 0)

    turned = []
    for b in range(3):
        total = jnp.zeros((2 * LANES, 2 * LANES), F32)
        for k in range(kernels):
            total += jnp.dot(row_bands_t[k], adjoint[b, k], preferred_element_type=F32)
        total = 2.0 * total
        rows = jnp.concatenate(
            [total[:LANES, :LANES], total[LANES:, :LANES] + total[:LANES, LANES:], total[LANES:, LANES:]], axis=0)
        turned.append(pltpu.roll(rows, ambit, 1))
    blocks = (jnp.where(low, turned[0], turned[1]), jnp.where(low, turned[1], turned[2]),
              jnp.where(low, turned[2], turned[0]))
    flag_rows = jnp.concatenate(
        [jnp.full((1, LANES), flags[g].astype(F32)) for g in range(tile_rows)]
        + [jnp.zeros((16 - tile_rows, LANES), F32)], axis=0)
    for q in range(pw_count):
        first = ambit + q * own_rows
        slot = lax.rem(q - place[0] + pw_count, pw_count)
        if q * own_rows < ambit:
            edge = ambit + tile + q * own_rows
        else:
            edge = max(q * own_rows - (tile - ambit), 0)
        for b, block in enumerate(blocks):
            main = block[first:first + own_rows].astype(BF16)
            side = block[edge:edge + edge_rows].astype(BF16)
            if b < 2:
                center[slot, 0:own_rows, b * LANES:(b + 1) * LANES] = main
                center[slot, own_rows:, b * LANES:(b + 1) * LANES] = side
            else:
                rims[slot, 0:own_rows, :] = main
                rims[slot, own_rows:pack_rows, :] = side
                rims[slot, pack_rows:, :] = flag_rows.astype(BF16)


def greet(devices, has_left, has_right, pw_count, partners):
    barrier = pltpu.get_barrier_semaphore()
    p, c = lax.axis_index("pw"), lax.axis_index("tile")
    for step in range(1, pw_count if partners else 1):
        pl.semaphore_signal(barrier, inc=1, device_id=(lax.rem(p + step, pw_count), c), device_id_type=MESH)
    for has, column in ((has_left, c - 1), (has_right, c + 1)):
        @pl.when(has)
        def _(column=column):
            for q in devices:
                pl.semaphore_signal(barrier, inc=1, device_id=(q, column), device_id_type=MESH)
    neighbours = jnp.where(has_left, 1, 0) + jnp.where(has_right, 1, 0)
    pl.semaphore_wait(barrier, neighbours * len(devices) + (pw_count - 1 if partners else 0))


def halo_kernel(tile_count, to_right, to_left, from_left, from_right, send, recv):
    p, c = lax.axis_index("pw"), lax.axis_index("tile")
    has_left, has_right = c > 0, c < tile_count - 1
    greet([p], has_left, has_right, 1, False)

    def copy(side, column):
        return pltpu.make_async_remote_copy(
            src_ref=(to_right, to_left)[side], dst_ref=(from_left, from_right)[side],
            send_sem=send.at[side], recv_sem=recv.at[side], device_id=(p, column), device_id_type=MESH)

    for has, side, column in ((has_right, 0, c + 1), (has_left, 1, c - 1)):
        @pl.when(has)
        def _(side=side, column=column):
            copy(side, column).start()
    for has, side, column in ((has_right, 0, c + 1), (has_left, 1, c - 1)):
        @pl.when(has)
        def _(side=side, column=column):
            copy(side, column).wait_send()
            copy(1 - side, column).wait_recv()


def exchange_kernel(
    pw_count, tile_count, center, rims, centers, lefts, rights,
    center_send, center_recv, rim_send_0, rim_recv_0, rim_send_1, rim_recv_1,
):
    p, c = lax.axis_index("pw"), lax.axis_index("tile")
    has_left, has_right = c > 0, c < tile_count - 1
    others = [lax.rem(p + step, pw_count) for step in range(pw_count)]
    greet(others, has_left, has_right, pw_count, True)
    rim_sems = ((rim_send_0, rim_recv_0), (rim_send_1, rim_recv_1))

    def center_copy(step):
        return pltpu.make_async_remote_copy(
            src_ref=center.at[step], dst_ref=centers.at[step - 1], send_sem=center_send.at[step],
            recv_sem=center_recv.at[step], device_id=(others[step], c), device_id_type=MESH)

    def rim_copy(step, side, column):
        return pltpu.make_async_remote_copy(
            src_ref=rims.at[step], dst_ref=(lefts, rights)[side].at[step], send_sem=rim_sems[side][0].at[step],
            recv_sem=rim_sems[side][1].at[step], device_id=(others[step], column), device_id_type=MESH)

    for step in range(1, pw_count):
        center_copy(step).start()
    for has, side, column in ((has_right, 0, c + 1), (has_left, 1, c - 1)):
        @pl.when(has)
        def _(side=side, column=column):
            for step in reversed(range(pw_count)):
                rim_copy(step, side, column).start()
    for step in range(1, pw_count):
        center_copy(step).wait_send()
        center_copy(step).wait_recv()
    for has, side, column in ((has_right, 0, c + 1), (has_left, 1, c - 1)):
        @pl.when(has)
        def _(side=side, column=column):
            for step in range(pw_count):
                rim_copy(step, side, column).wait_send()
                rim_copy(step, 1 - side, column).wait_recv()


def gather_kernel(sizes, flags, place, own_center, centers, lefts, rights, out_ref):
    pw_count, tile_count, tile_rows, tile, ambit = sizes
    own_rows = tile // pw_count
    edge_rows = min(own_rows, ambit)
    pack_rows = own_rows + edge_rows
    p = place[0]
    c = place[1]
    total = own_center[0].astype(F32)
    for step in range(pw_count - 1):
        total += centers[step].astype(F32)
    left, right = lefts[0].astype(F32), rights[0].astype(F32)
    left_sum = sum(lefts[step, 0:pack_rows, :].astype(F32) for step in range(pw_count))
    right_sum = sum(rights[step, 0:pack_rows, :].astype(F32) for step in range(pw_count))
    left, left_sum = (jnp.where(c > 0, value, 0.0) for value in (left, left_sum))
    right, right_sum = (jnp.where(c < tile_count - 1, value, 0.0) for value in (right, right_sum))
    pack_low = low_lanes(pack_rows, ambit)
    left_sum = jnp.where(pack_low, left_sum, 0.0)
    right_sum = jnp.where(pack_low, 0.0, right_sum)
    is_low = jnp.where(p * own_rows < ambit, 1.0, 0.0).astype(F32)
    is_high = jnp.where((p + 1) * own_rows > tile - ambit, 1.0, 0.0).astype(F32)
    halves = ((total[:, :LANES], left_sum, left), (total[:, LANES:], right_sum, right))

    def flag_of(kind, g):
        if g < 0 or g >= tile_rows:
            return None
        if kind is None:
            return flags[g].astype(F32)
        return kind[pack_rows + g:pack_rows + g + 1, :]

    for b, (own, rim, rim_flags) in enumerate(halves):
        lanes = slice(b * LANES, (b + 1) * LANES)
        for g in range(tile_rows):
            out_ref[g, :, lanes] = (
                flag_of(None, g) * own[:own_rows] + flag_of(rim_flags, g) * rim[:own_rows])
            for at, switch, source in ((0, is_low, g - 1), (own_rows - edge_rows, is_high, g + 1)):
                if 0 <= source < tile_rows:
                    out_ref[g, at:at + edge_rows, lanes] += switch * (
                        flag_of(None, source) * own[own_rows:] + flag_of(rim_flags, source) * rim[own_rows:])


def solution(mesh):
    pw_count, tile_count = mesh.shape["pw"], mesh.shape["tile"]

    def on_device(mask_tiles, target_print, geometry_flags, kernel_taps, dose_factor):
        tile_rows, tile, _ = mask_tiles.shape
        kernels, kinds, tap_count = kernel_taps.shape[1:]
        ambit = (tap_count - 1) // 2
        height, extent = tile_rows * tile, tile + 2 * ambit
        own_rows = tile // pw_count
        pack_rows = own_rows + min(own_rows, ambit)
        wide = 2 * LANES
        vmem = pl.BlockSpec(memory_space=pltpu.VMEM)
        smem = pl.BlockSpec(memory_space=pltpu.SMEM)
        anywhere = pl.BlockSpec(memory_space=pl.ANY)
        p = lax.axis_index("pw")
        taps = jnp.pad(kernel_taps[0], ((0, 0), (0, 8 - kinds), (0, wide - tap_count)))
        flags = geometry_flags.reshape(tile_rows)
        mask = mask_tiles.reshape(height, tile)
        c = lax.axis_index("tile")
        place = jnp.stack([p, c]).astype(jnp.int32)
        half = height // 2
        rim_type = jax.ShapeDtypeStruct((half, LANES), BF16)

        def packed(columns):
            return jnp.concatenate([columns[:half], columns[half:]], axis=1).astype(BF16)

        def unpacked(rim):
            return jnp.concatenate([rim[:, :ambit], rim[:, ambit:]], axis=0)

        def halo(*refs):
            halo_kernel(tile_count, *refs)

        before, after = pl.pallas_call(
            halo,
            out_shape=(rim_type, rim_type),
            in_specs=[anywhere] * 2,
            out_specs=(anywhere,) * 2,
            scratch_shapes=[pltpu.SemaphoreType.DMA((2,))] * 2,
            compiler_params=pltpu.CompilerParams(collective_id=1, has_side_effects=True),
        )(packed(mask[:, tile - ambit:]), packed(mask[:, :ambit]))
        before = jnp.where(c > 0, before, jnp.zeros_like(before))
        after = jnp.where(c < tile_count - 1, after, jnp.zeros_like(after))
        halos = jnp.pad(jnp.concatenate([unpacked(before), unpacked(after)], axis=1), ((ambit, ambit), (0, 0)))

        def gradient(*refs):
            gradient_kernel((pw_count, tile_rows, tile, kernels, ambit), *refs)

        def gather(*refs):
            gather_kernel((pw_count, tile_count, tile_rows, tile, ambit), *refs)

        center, rims = pl.pallas_call(
            gradient,
            out_shape=(
                jax.ShapeDtypeStruct((pw_count, pack_rows, tile), BF16),
                jax.ShapeDtypeStruct((pw_count, pack_rows + 16, LANES), BF16),
            ),
            in_specs=[anywhere, anywhere, smem, vmem, smem, smem, vmem],
            out_specs=(vmem, vmem),
            scratch_shapes=[
                pltpu.VMEM((height + 2 * ambit, tile), F32),
                pltpu.VMEM((tile, tile), F32),
                pltpu.VMEM((kernels, wide, wide), BF16),
                pltpu.VMEM((kernels, wide, wide), BF16),
                pltpu.VMEM((kernels, wide, wide), BF16),
                pltpu.VMEM((kernels, wide, wide), BF16),
                pltpu.VMEM((kernels, 2, tile, extent), BF16),
                pltpu.VMEM((kernels, 2 * tile, wide), F32),
                pltpu.VMEM((2 * tile, LANES), F32),
                pltpu.VMEM((3, kernels, wide, wide), BF16),
                pltpu.SemaphoreType.DMA((2,)),
            ],
            compiler_params=pltpu.CompilerParams(vmem_limit_bytes=48 * 1024 * 1024),
        )(mask, target_print, flags, taps, dose_factor, place, halos)

        def exchange(*refs):
            exchange_kernel(pw_count, tile_count, *refs)

        centers, lefts, rights = pl.pallas_call(
            exchange,
            out_shape=(
                jax.ShapeDtypeStruct((pw_count - 1, pack_rows, tile), BF16),
                jax.ShapeDtypeStruct((pw_count, pack_rows + 16, LANES), BF16),
                jax.ShapeDtypeStruct((pw_count, pack_rows + 16, LANES), BF16),
            ),
            in_specs=[anywhere] * 2,
            out_specs=(anywhere,) * 3,
            scratch_shapes=[pltpu.SemaphoreType.DMA((pw_count,))] * 6,
            compiler_params=pltpu.CompilerParams(collective_id=2, has_side_effects=True),
        )(center, rims)
        return pl.pallas_call(
            gather,
            out_shape=jax.ShapeDtypeStruct((tile_rows, own_rows, tile), F32),
            in_specs=[smem, smem] + [vmem] * 4,
            out_specs=vmem,
        )(flags, place, center, centers, lefts, rights)

    return jax.shard_map(
        on_device,
        mesh=mesh,
        in_specs=(
            P(None, None, "tile"),
            P(None, None, "tile"),
            P(None, "tile"),
            P("pw", None, None, None),
            P("pw"),
        ),
        out_specs=P(None, "pw", "tile"),
        check_vma=False,
    )
```
